32 devices in a mesh: replica: 4 (over y, x), shard: 8 (over z, core).
Axes of the slice: x: 2, y: 2, z: 4, core: 2. Of those that a mesh axis runs over, the one named last changes fastest.
Arguments:
- block_input: float32 [32, 224, 768], P(('replica', 'shard')), may hold values from -6 to 6
- out_cotangent: float32 [32, 224, 768], P(('replica', 'shard')), may hold values from -6 to 6
- ln1_gain: bfloat16 [768], P('shard'), may hold values from 0.5 to 1.5
- ln1_bias: bfloat16 [768], P('shard'), may hold values from -3 to 3
- attn_query: bfloat16 [768, 768], P('shard'), as said below
- query_bias: bfloat16 [768], P('shard'), may hold values from -3 to 3
- attn_key: bfloat16 [768, 768], P('shard'), may hold values from -0.21875 to 0.21875
- attn_value: bfloat16 [768, 768], P('shard'), may hold values from -0.21875 to 0.21875
- value_bias: bfloat16 [768], P('shard'), may hold values from -3 to 3
- attn_out: bfloat16 [768, 768], P('shard'), may hold values from -2 to 2
- out_bias: bfloat16 [768], P('shard'), may hold values from -3 to 3
- ln2_gain: bfloat16 [768], P('shard'), may hold values from 0.5 to 1.5
- ln2_bias: bfloat16 [768], P('shard'), may hold values from -3 to 3
- fc1_weight: bfloat16 [768, 3072], P('shard'), may hold values from -0.21875 to 0.21875
- fc1_bias: bfloat16 [3072], P('shard'), may hold values from -3 to 3
- fc2_weight: bfloat16 [3072, 768], P('shard'), may hold values from -0.21875 to 0.21875
- fc2_bias: bfloat16 [768], P('shard'), may hold values from -3 to 3
Outputs:
- block_output: float32 [32, 224, 768], P(('replica', 'shard'))
- input_grad: float32 [32, 224, 768], P(('replica', 'shard'))
- ln1_gain_grad: float32 [768], P('shard')
- ln1_bias_grad: float32 [768], P('shard')
- query_grad: float32 [768, 768], P('shard')
- query_bias_grad: float32 [768], P('shard')
- key_grad: float32 [768, 768], P('shard')
- value_grad: float32 [768, 768], P('shard')
- value_bias_grad: float32 [768], P('shard')
- out_grad: float32 [768, 768], P('shard')
- out_bias_grad: float32 [768], P('shard')
- ln2_gain_grad: float32 [768], P('shard')
- ln2_bias_grad: float32 [768], P('shard')
- fc1_grad: float32 [768, 3072], P('shard')
- fc1_bias_grad: float32 [3072], P('shard')
- fc2_grad: float32 [3072, 768], P('shard')
- fc2_bias_grad: float32 [768], P('shard')
The draws below stay inside these ranges and needn't reach their ends.
Inputs may be any that keep to these rules, and one draw needn't show every extreme that they name: `attn_query`: weights of the query projection.
All inputs are finite; a program needn't handle non-finite values.
Results may differ from the reference program's by a relative error of at most 0.014.
The reference program's roundings to bfloat16 on the way (of `act1`, `mixed`, `act2`, `activ`, `grad_mixed` and `grad_scores`) count: a program that leaves them out, or rounds other values in their place, can miss the bound.
Values may be sent and summed in bfloat16 or wider, within the bound.
A program may use at most 128 MiB of HBM per device.

```python
import math
import jax
import jax.numpy as jnp
from jax import lax

D = 768
HEADS = 12
HEAD_DIM = 64
FF = 3072
FRAMES = 224
CLIPS = 32


def draw_attn_query(key, part):
    base = jax.random.truncated_normal(key, -4.0, 4.0, (D, D), jnp.float32) / math.sqrt(D)
    return base.astype(jnp.bfloat16)


def block_levels(stream_key, shape, shards, low, high):
    def one(dim, shards_of):
        steps = jax.random.uniform(jax.random.fold_in(jax.random.fold_in(stream_key, 6), dim), (shards_of,), jnp.float32, low / len(shards), high / len(shards))
        return jnp.repeat(jnp.exp(steps), shape[dim] // shards_of).reshape((-1,) + (1,) * (len(shape) - dim - 1))

    level = one(*shards[0])
    for cut in shards[1:]:
        level = level * one(*cut)
    return level


def noise(key, dims, scale, bound, split=(), held_as=jnp.bfloat16):
    loudness = block_levels(key, dims, split, -0.22, 0.18) if split else 1.0
    array = jax.random.normal(key, dims, jnp.float32) * scale * loudness
    return jnp.minimum(jnp.maximum(array, -bound), bound).astype(held_as)


def setup_inputs(seed: int = 0) -> dict:
    key_of = jax.random.split(jax.random.key(seed), 18)
    return {
        "block_input": noise(key_of[0], (CLIPS, FRAMES, D), 1.0, 6.0, ((0, 32),), jnp.float32),
        "out_cotangent": noise(key_of[1], (CLIPS, FRAMES, D), 1.0, 6.0, ((0, 32),), jnp.float32),
        "ln1_gain": jnp.clip(1.0 + 0.1 * jax.random.normal(key_of[2], (D,), jnp.float32), 0.5, 1.5).astype(jnp.bfloat16),
        "ln1_bias": noise(key_of[3], (D,), 0.5, 3.0, ((0, 8),)),
        "attn_query": draw_attn_query(jax.random.fold_in(key_of[17], 71), 0),
        "query_bias": noise(key_of[5], (D,), 0.5, 3.0, ((0, 8),)),
        "attn_key": noise(key_of[6], (D, D), D ** -0.5, 0.21875, ((0, 8),)),
        "attn_value": noise(key_of[7], (D, D), D ** -0.5, 0.21875, ((0, 8),)),
        "value_bias": noise(key_of[8], (D,), 0.5, 3.0, ((0, 8),)),
        "attn_out": noise(key_of[9], (D, D), (HEAD_DIM // 8) ** -0.5, 2.0, ((0, 8),)),
        "out_bias": noise(key_of[10], (D,), 0.5, 3.0, ((0, 8),)),
        "ln2_gain": jnp.clip(1.0 + 0.1 * jax.random.normal(key_of[11], (D,), jnp.float32), 0.5, 1.5).astype(jnp.bfloat16),
        "ln2_bias": noise(key_of[12], (D,), 0.5, 3.0, ((0, 8),)),
        "fc1_weight": noise(key_of[13], (D, FF), D ** -0.5, 0.21875, ((0, 8),)),
        "fc1_bias": noise(key_of[14], (FF,), 0.5, 3.0, ((0, 8),)),
        "fc2_weight": noise(key_of[15], (FF, D), (FF // 4) ** -0.5, 0.21875, ((0, 8),)),
        "fc2_bias": noise(key_of[16], (D,), 0.5, 3.0, ((0, 8),)),
    }


def matmul(spec, left, right):
    return jnp.einsum(spec, left.astype(jnp.float32), right.astype(jnp.float32))

def normalize(inputs, gain, shift):
    center = inputs - lax.optimization_barrier(jnp.mean(inputs, axis=-1, keepdims=True))
    inv_std = lax.rsqrt(lax.optimization_barrier(jnp.mean(center * center, axis=-1, keepdims=True)) + 1e-05)
    normed = center * inv_std
    act = (normed * gain.astype(jnp.float32) + shift.astype(jnp.float32)).astype(jnp.bfloat16)
    return (normed, inv_std, act)

def norm_back(grad_out, normed, inv_std, gain):
    scaled = grad_out * gain.astype(jnp.float32)
    return inv_std * (scaled - lax.optimization_barrier(jnp.mean(scaled, axis=-1, keepdims=True)) - normed * lax.optimization_barrier(jnp.mean(scaled * normed, axis=-1, keepdims=True)))

def gelu_parts(pre):
    cdf = 0.5 * (1.0 + jax.scipy.special.erf(pre * 0.7071067811865476))
    dens = jnp.exp(-0.5 * pre * pre) * 0.3989422804014327
    return (pre * cdf, cdf + pre * dens)

def layer_pass(block_input, out_cotangent, weights):
    ln1_gain, ln1_bias, attn_query, query_bias, attn_key, attn_value, value_bias, attn_out, out_bias, ln2_gain, ln2_bias, fc1_weight, fc1_bias, fc2_weight, fc2_bias = weights
    f32 = jnp.float32
    bf16 = jnp.bfloat16
    clips, frames, width = block_input.shape
    scale = HEAD_DIM ** (-0.5)
    heads_shape = (clips, frames, HEADS, HEAD_DIM)
    normed1, inv1, act1 = normalize(block_input, ln1_gain, ln1_bias)
    query = ((matmul('cld,de->cle', act1, attn_query) + query_bias.astype(f32)) * scale).astype(bf16).reshape(heads_shape)
    keys = matmul('cld,de->cle', act1, attn_key).astype(bf16).reshape(heads_shape)
    values = (matmul('cld,de->cle', act1, attn_value) + value_bias.astype(f32)).astype(bf16).reshape(heads_shape)
    scores = matmul('clhe,cmhe->chlm', query, keys)
    top = lax.optimization_barrier(jnp.max(scores, axis=-1, keepdims=True))
    log_total = top + jnp.log(lax.optimization_barrier(jnp.sum(jnp.exp(scores - top), axis=-1, keepdims=True)))
    probs = jnp.exp(scores - log_total)
    mixed = matmul('chlm,cmhe->clhe', probs.astype(bf16), values).astype(bf16).reshape(clips, frames, width)
    middle = block_input + matmul('cld,de->cle', mixed, attn_out) + out_bias.astype(f32)
    normed2, inv2, act2 = normalize(middle, ln2_gain, ln2_bias)
    pre = matmul('cld,df->clf', act2, fc1_weight) + fc1_bias.astype(f32)
    activ, slope = gelu_parts(pre)
    activ_b = activ.astype(bf16)
    block_output = middle + matmul('clf,fd->cld', activ_b, fc2_weight) + fc2_bias.astype(f32)
    grad_b = out_cotangent.astype(bf16)
    fc2_grad = matmul('clf,cld->fd', activ_b, grad_b)
    fc2_bias_grad = lax.optimization_barrier(jnp.sum(out_cotangent, axis=(0, 1)))
    grad_pre = matmul('cld,fd->clf', grad_b, fc2_weight) * slope
    grad_pre_b = grad_pre.astype(bf16)
    fc1_grad = matmul('cld,clf->df', act2, grad_pre_b)
    fc1_bias_grad = lax.optimization_barrier(jnp.sum(grad_pre, axis=(0, 1)))
    grad_act2 = matmul('clf,df->cld', grad_pre_b, fc1_weight)
    ln2_gain_grad = lax.optimization_barrier(jnp.sum(grad_act2 * normed2, axis=(0, 1)))
    ln2_bias_grad = lax.optimization_barrier(jnp.sum(grad_act2, axis=(0, 1)))
    grad_middle = out_cotangent + norm_back(grad_act2, normed2, inv2, ln2_gain)
    grad_mid_b = grad_middle.astype(bf16)
    out_grad = matmul('cld,cle->de', mixed, grad_mid_b)
    out_bias_grad = lax.optimization_barrier(jnp.sum(grad_middle, axis=(0, 1)))
    grad_mixed = matmul('cle,de->cld', grad_mid_b, attn_out).astype(bf16).reshape(heads_shape)
    again = jnp.exp(matmul('clhe,cmhe->chlm', query, keys) - log_total)
    grad_probs = matmul('clhe,cmhe->chlm', grad_mixed, values)
    inner = lax.optimization_barrier(jnp.sum(again * grad_probs, axis=-1, keepdims=True))
    grad_scores = (again * (grad_probs - inner)).astype(bf16)
    grad_query = matmul('chlm,cmhe->clhe', grad_scores, keys).reshape(clips, frames, width) * scale
    grad_keys = matmul('chlm,clhe->cmhe', grad_scores, query).reshape(clips, frames, width)
    grad_values = matmul('chlm,clhe->cmhe', again.astype(bf16), grad_mixed).reshape(clips, frames, width)
    query_bias_grad = lax.optimization_barrier(jnp.sum(grad_query, axis=(0, 1)))
    value_bias_grad = lax.optimization_barrier(jnp.sum(grad_values, axis=(0, 1)))
    grad_query_b = grad_query.astype(bf16)
    grad_keys_b = grad_keys.astype(bf16)
    grad_values_b = grad_values.astype(bf16)
    query_grad = matmul('cld,cle->de', act1, grad_query_b)
    key_grad = matmul('cld,cle->de', act1, grad_keys_b)
    value_grad = matmul('cld,cle->de', act1, grad_values_b)
    grad_act1 = matmul('cle,de->cld', grad_query_b, attn_query) + matmul('cle,de->cld', grad_keys_b, attn_key) + matmul('cle,de->cld', grad_values_b, attn_value)
    ln1_gain_grad = lax.optimization_barrier(jnp.sum(grad_act1 * normed1, axis=(0, 1)))
    ln1_bias_grad = lax.optimization_barrier(jnp.sum(grad_act1, axis=(0, 1)))
    input_grad = grad_middle + norm_back(grad_act1, normed1, inv1, ln1_gain)
    grads = (ln1_gain_grad, ln1_bias_grad, query_grad, query_bias_grad, key_grad, value_grad, value_bias_grad, out_grad, out_bias_grad, ln2_gain_grad, ln2_bias_grad, fc1_grad, fc1_bias_grad, fc2_grad, fc2_bias_grad)
    return (block_output, input_grad, grads)

def reference(block_input, out_cotangent, ln1_gain, ln1_bias, attn_query, query_bias, attn_key, attn_value, value_bias, attn_out, out_bias, ln2_gain, ln2_bias, fc1_weight, fc1_bias, fc2_weight, fc2_bias):
    weights = (ln1_gain, ln1_bias, attn_query, query_bias, attn_key, attn_value, value_bias, attn_out, out_bias, ln2_gain, ln2_bias, fc1_weight, fc1_bias, fc2_weight, fc2_bias)

    def one_clip(carry, pair):
        output, grad_in, grads = layer_pass(pair[0][None], pair[1][None], weights)
        summed = tuple((total + grad for total, grad in zip(carry, grads)))
        return (summed, (output[0], grad_in[0]))
    start = tuple((jnp.zeros(weight.shape, jnp.float32) for weight in weights))
    totals, outputs = lax.scan(one_clip, start, (block_input, out_cotangent))
    return (outputs[0], outputs[1], totals[0], totals[1], totals[2], totals[3], totals[4], totals[5], totals[6], totals[7], totals[8], totals[9], totals[10], totals[11], totals[12], totals[13], totals[14])
```

```python
import jax
import jax.numpy as jnp
from jax import lax
from jax.sharding import PartitionSpec as P

HEADS = 12
HEAD_DIM = 64


def matmul(spec, left, right):
    return jnp.einsum(spec, left, right, preferred_element_type=jnp.float32)


def normalize(inputs, gain, shift):
    center = inputs - jnp.mean(inputs, axis=-1, keepdims=True)
    inv_std = lax.rsqrt(jnp.mean(center * center, axis=-1, keepdims=True) + 1e-05)
    normed = center * inv_std
    act = (normed * gain.astype(jnp.float32) + shift.astype(jnp.float32)).astype(jnp.bfloat16)
    return (normed, inv_std, act)


def norm_back(grad_out, normed, inv_std, gain):
    scaled = grad_out * gain.astype(jnp.float32)
    return inv_std * (
        scaled
        - jnp.mean(scaled, axis=-1, keepdims=True)
        - normed * jnp.mean(scaled * normed, axis=-1, keepdims=True)
    )


def gelu_parts(pre):
    cdf = 0.5 * (1.0 + jax.scipy.special.erf(pre * 0.7071067811865476))
    dens = jnp.exp(-0.5 * pre * pre) * 0.3989422804014327
    return (pre * cdf, cdf + pre * dens)


def forward_pass(block_input, attn_full, mlp_full):
    ln1_gain, ln1_bias, attn_qkv, query_bias, value_bias, attn_out, out_bias = attn_full
    ln2_gain, ln2_bias, fc1_weight, fc1_bias, fc2_weight, fc2_bias = mlp_full
    f32 = jnp.float32
    bf16 = jnp.bfloat16
    clips, frames, width = block_input.shape
    scale = HEAD_DIM ** (-0.5)
    heads_shape = (clips, frames, HEADS, HEAD_DIM)
    normed1, inv1, act1 = normalize(block_input, ln1_gain, ln1_bias)
    mixed_in = matmul("cld,de->cle", act1, attn_qkv)
    query = ((mixed_in[..., :width] + query_bias.astype(f32)) * scale).astype(bf16)
    keys = mixed_in[..., width : 2 * width].astype(bf16)
    values = (mixed_in[..., 2 * width :] + value_bias.astype(f32)).astype(bf16)
    query, keys, values = (part.reshape(heads_shape) for part in (query, keys, values))
    scores = matmul("clhe,cmhe->chlm", query, keys)
    top = jnp.max(scores, axis=-1, keepdims=True)
    log_total = top + jnp.log(jnp.sum(jnp.exp(scores - top), axis=-1, keepdims=True))
    probs = jnp.exp(scores - log_total)
    mixed = (
        matmul("chlm,cmhe->clhe", probs.astype(bf16), values)
        .astype(bf16)
        .reshape(clips, frames, width)
    )
    middle = block_input + matmul("cld,de->cle", mixed, attn_out) + out_bias.astype(f32)
    normed2, inv2, act2 = normalize(middle, ln2_gain, ln2_bias)
    pre = matmul("cld,df->clf", act2, fc1_weight) + fc1_bias.astype(f32)
    activ, slope = gelu_parts(pre)
    activ_b = activ.astype(bf16)
    block_output = middle + matmul("clf,fd->cld", activ_b, fc2_weight) + fc2_bias.astype(f32)
    saved = (
        normed1,
        inv1,
        act1,
        query,
        keys,
        values,
        log_total,
        mixed,
        normed2,
        inv2,
        act2,
        slope,
        activ_b,
    )
    return (block_output, saved)


def backward_pass(out_cotangent, saved, attn_full, mlp_full):
    ln1_gain, ln1_bias, attn_qkv, query_bias, value_bias, attn_out, out_bias = attn_full
    ln2_gain, ln2_bias, fc1_weight, fc1_bias, fc2_weight, fc2_bias = mlp_full
    (
        normed1,
        inv1,
        act1,
        query,
        keys,
        values,
        log_total,
        mixed,
        normed2,
        inv2,
        act2,
        slope,
        activ_b,
    ) = saved
    bf16 = jnp.bfloat16
    clips, frames, width = out_cotangent.shape
    scale = HEAD_DIM ** (-0.5)
    heads_shape = (clips, frames, HEADS, HEAD_DIM)
    grad_b = out_cotangent.astype(bf16)
    fc2_grad = matmul("clf,cld->fd", activ_b, grad_b)
    fc2_bias_grad = jnp.sum(out_cotangent, axis=(0, 1))
    grad_pre = matmul("cld,fd->clf", grad_b, fc2_weight) * slope
    grad_pre_b = grad_pre.astype(bf16)
    fc1_grad = matmul("cld,clf->df", act2, grad_pre_b)
    fc1_bias_grad = jnp.sum(grad_pre, axis=(0, 1))
    grad_act2 = matmul("clf,df->cld", grad_pre_b, fc1_weight)
    ln2_gain_grad = jnp.sum(grad_act2 * normed2, axis=(0, 1))
    ln2_bias_grad = jnp.sum(grad_act2, axis=(0, 1))
    grad_middle = out_cotangent + norm_back(grad_act2, normed2, inv2, ln2_gain)
    grad_mid_b = grad_middle.astype(bf16)
    out_grad = matmul("cld,cle->de", mixed, grad_mid_b)
    out_bias_grad = jnp.sum(grad_middle, axis=(0, 1))
    grad_mixed = matmul("cle,de->cld", grad_mid_b, attn_out).astype(bf16).reshape(heads_shape)
    again = jnp.exp(matmul("clhe,cmhe->chlm", query, keys) - log_total)
    grad_probs = matmul("clhe,cmhe->chlm", grad_mixed, values)
    inner = jnp.sum(again * grad_probs, axis=-1, keepdims=True)
    grad_scores = (again * (grad_probs - inner)).astype(bf16)
    grad_query = matmul("chlm,cmhe->clhe", grad_scores, keys).reshape(clips, frames, width) * scale
    grad_keys = matmul("chlm,clhe->cmhe", grad_scores, query).reshape(clips, frames, width)
    grad_values = matmul("chlm,clhe->cmhe", again.astype(bf16), grad_mixed).reshape(
        clips, frames, width
    )
    query_bias_grad = jnp.sum(grad_query, axis=(0, 1))
    value_bias_grad = jnp.sum(grad_values, axis=(0, 1))
    grad_query_b = grad_query.astype(bf16)
    grad_keys_b = grad_keys.astype(bf16)
    grad_values_b = grad_values.astype(bf16)
    joined = jnp.concatenate((grad_query_b, grad_keys_b, grad_values_b), axis=-1)
    qkv_grad = matmul("cld,cle->de", act1, joined)
    grad_act1 = matmul("cle,de->cld", joined, attn_qkv)
    ln1_gain_grad = jnp.sum(grad_act1 * normed1, axis=(0, 1))
    ln1_bias_grad = jnp.sum(grad_act1, axis=(0, 1))
    input_grad = grad_middle + norm_back(grad_act1, normed1, inv1, ln1_gain)
    attn_grads = (
        ln1_gain_grad,
        ln1_bias_grad,
        qkv_grad,
        query_bias_grad,
        value_bias_grad,
        out_grad,
        out_bias_grad,
    )
    mlp_grads = (ln2_gain_grad, ln2_bias_grad, fc1_grad, fc1_bias_grad, fc2_grad, fc2_bias_grad)
    return (input_grad, attn_grads, mlp_grads)


def body(
    block_input,
    out_cotangent,
    ln1_gain,
    ln1_bias,
    attn_query,
    query_bias,
    attn_key,
    attn_value,
    value_bias,
    attn_out,
    out_bias,
    ln2_gain,
    ln2_bias,
    fc1_weight,
    fc1_bias,
    fc2_weight,
    fc2_bias,
):
    f32 = jnp.float32
    bf16 = jnp.bfloat16
    rows, width = attn_query.shape
    per_row = fc1_bias.shape[0] // rows
    narrow = (
        ln1_gain,
        ln1_bias,
        query_bias,
        value_bias,
        out_bias,
        ln2_gain,
        ln2_bias,
        fc2_bias,
    )
    columns = jnp.concatenate(
        (jnp.stack(narrow, axis=1), fc1_bias.reshape(rows, per_row)), axis=1
    )
    used = columns.shape[1]
    spare = -used % 128
    packed = jnp.concatenate(
        (attn_query, attn_key, attn_value, attn_out, jnp.pad(columns, ((0, 0), (0, spare)))),
        axis=1,
    )
    attn_all = lax.all_gather(packed, "shard", axis=0, tiled=True)
    fc1_all = lax.all_gather(fc1_weight, "shard", axis=0, tiled=True)
    fc2_all = lax.all_gather(fc2_weight, "shard", axis=0, tiled=True)
    small = attn_all[:, 4 * width : 4 * width + used]
    g1, b1, bq, bv, bo, g2, b2, bf2 = (small[:, i] for i in range(len(narrow)))
    bf1 = small[:, len(narrow) :].reshape(-1)
    attn_full = (g1, b1, attn_all[:, : 3 * width], bq, bv, attn_all[:, 3 * width : 4 * width], bo)
    mlp_full = (g2, b2, fc1_all, bf1, fc2_all, bf2)
    block_output, saved = forward_pass(block_input, attn_full, mlp_full)
    input_grad, attn_grads, mlp_grads = backward_pass(out_cotangent, saved, attn_full, mlp_full)
    dg1, db1, dqkv, dbq, dbv, dout, dbo = attn_grads
    dg2, db2, dfc1, dbf1, dfc2, dbf2 = mlp_grads

    def owned(grad):
        part = lax.psum_scatter(grad.astype(bf16), "shard", scatter_dimension=0, tiled=True)
        return lax.psum(part, "replica").astype(f32)

    fc2_owned = owned(dfc2)
    fc1_owned = owned(dfc1)
    thin = jnp.concatenate(
        (
            jnp.stack((dg1, db1, dbq, dbv, dbo, dg2, db2, dbf2), axis=1),
            dbf1.reshape(-1, per_row),
        ),
        axis=1,
    )
    attn_owned = owned(
        jnp.concatenate((dqkv, dout, jnp.pad(thin, ((0, 0), (0, spare)))), axis=1)
    )
    base = 4 * width
    og1, ob1, obq, obv, obo, og2, ob2, obf2 = (
        attn_owned[:, base + i] for i in range(len(narrow))
    )
    obf1 = attn_owned[:, base + len(narrow) : base + used].reshape(-1)
    return (
        block_output,
        input_grad,
        og1,
        ob1,
        attn_owned[:, :width],
        obq,
        attn_owned[:, width : 2 * width],
        attn_owned[:, 2 * width : 3 * width],
        obv,
        attn_owned[:, 3 * width : 4 * width],
        obo,
        og2,
        ob2,
        fc1_owned,
        obf1,
        fc2_owned,
        obf2,
    )


def solution(mesh):
    placed = (
        P(("replica", "shard"), None, None),
        P(("replica", "shard"), None, None),
        P("shard"),
        P("shard"),
        P("shard", None),
        P("shard"),
        P("shard", None),
        P("shard", None),
        P("shard"),
        P("shard", None),
        P("shard"),
        P("shard"),
        P("shard"),
        P("shard", None),
        P("shard"),
        P("shard", None),
        P("shard"),
    )
    return jax.shard_map(
        body,
        mesh=mesh,
        in_specs=placed,
        out_specs=(
            P(("replica", "shard"), None, None),
            P(("replica", "shard"), None, None),
            P("shard"),
            P("shard"),
            P("shard", None),
            P("shard"),
            P("shard", None),
            P("shard", None),
            P("shard"),
            P("shard", None),
            P("shard"),
            P("shard"),
            P("shard"),
            P("shard", None),
            P("shard"),
            P("shard", None),
            P("shard"),
        ),
        check_vma=False,
    )
```

```python
import jax
import jax.numpy as jnp
from jax import lax
from jax.sharding import PartitionSpec as P

HEADS = 12
HEAD_DIM = 64


def matmul(spec, left, right):
    return jnp.einsum(spec, left, right, preferred_element_type=jnp.float32)


def normalize(inputs, gain, shift):
    center = inputs - jnp.mean(inputs, axis=-1, keepdims=True)
    inv_std = lax.rsqrt(jnp.mean(center * center, axis=-1, keepdims=True) + 1e-05)
    normed = center * inv_std
    act = (normed * gain.astype(jnp.float32) + shift.astype(jnp.float32)).astype(jnp.bfloat16)
    return (normed, inv_std, act)


def norm_back(grad_out, normed, inv_std, gain):
    scaled = grad_out * gain.astype(jnp.float32)
    return inv_std * (
        scaled
        - jnp.mean(scaled, axis=-1, keepdims=True)
        - normed * jnp.mean(scaled * normed, axis=-1, keepdims=True)
    )


def gelu_parts(pre):
    cdf = 0.5 * (1.0 + jax.scipy.special.erf(pre * 0.7071067811865476))
    dens = jnp.exp(-0.5 * pre * pre) * 0.3989422804014327
    return (pre * cdf, cdf + pre * dens)


def forward_pass(block_input, attn_full, mlp_full):
    ln1_gain, ln1_bias, attn_qkv, query_bias, value_bias, attn_out, out_bias = attn_full
    ln2_gain, ln2_bias, fc1_weight, fc1_bias, fc2_weight, fc2_bias = mlp_full
    f32 = jnp.float32
    bf16 = jnp.bfloat16
    clips, frames, width = block_input.shape
    scale = HEAD_DIM ** (-0.5)
    heads_shape = (clips, frames, HEADS, HEAD_DIM)
    normed1, inv1, act1 = normalize(block_input, ln1_gain, ln1_bias)
    mixed_in = matmul("cld,de->cle", act1, attn_qkv)
    query = ((mixed_in[..., :width] + query_bias.astype(f32)) * scale).astype(bf16)
    keys = mixed_in[..., width : 2 * width].astype(bf16)
    values = (mixed_in[..., 2 * width :] + value_bias.astype(f32)).astype(bf16)
    query, keys, values = (part.reshape(heads_shape) for part in (query, keys, values))
    scores = matmul("clhe,cmhe->chlm", query, keys)
    top = jnp.max(scores, axis=-1, keepdims=True)
    log_total = top + jnp.log(jnp.sum(jnp.exp(scores - top), axis=-1, keepdims=True))
    probs = jnp.exp(scores - log_total)
    mixed = (
        matmul("chlm,cmhe->clhe", probs.astype(bf16), values)
        .astype(bf16)
        .reshape(clips, frames, width)
    )
    middle = block_input + matmul("cld,de->cle", mixed, attn_out) + out_bias.astype(f32)
    normed2, inv2, act2 = normalize(middle, ln2_gain, ln2_bias)
    pre = matmul("cld,df->clf", act2, fc1_weight) + fc1_bias.astype(f32)
    activ, slope = gelu_parts(pre)
    activ_b = activ.astype(bf16)
    block_output = middle + matmul("clf,fd->cld", activ_b, fc2_weight) + fc2_bias.astype(f32)
    saved = (
        normed1,
        inv1,
        act1,
        query,
        keys,
        values,
        log_total,
        mixed,
        normed2,
        inv2,
        act2,
        slope,
        activ_b,
    )
    return (block_output, saved)


def backward_pass(out_cotangent, saved, attn_full, mlp_full):
    ln1_gain, ln1_bias, attn_qkv, query_bias, value_bias, attn_out, out_bias = attn_full
    ln2_gain, ln2_bias, fc1_weight, fc1_bias, fc2_weight, fc2_bias = mlp_full
    (
        normed1,
        inv1,
        act1,
        query,
        keys,
        values,
        log_total,
        mixed,
        normed2,
        inv2,
        act2,
        slope,
        activ_b,
    ) = saved
    bf16 = jnp.bfloat16
    clips, frames, width = out_cotangent.shape
    scale = HEAD_DIM ** (-0.5)
    heads_shape = (clips, frames, HEADS, HEAD_DIM)
    grad_b = out_cotangent.astype(bf16)
    fc2_grad = matmul("clf,cld->fd", activ_b, grad_b)
    fc2_bias_grad = jnp.sum(out_cotangent, axis=(0, 1))
    grad_pre = matmul("cld,fd->clf", grad_b, fc2_weight) * slope
    grad_pre_b = grad_pre.astype(bf16)
    fc1_grad = matmul("cld,clf->df", act2, grad_pre_b)
    fc1_bias_grad = jnp.sum(grad_pre, axis=(0, 1))
    grad_act2 = matmul("clf,df->cld", grad_pre_b, fc1_weight)
    ln2_gain_grad = jnp.sum(grad_act2 * normed2, axis=(0, 1))
    ln2_bias_grad = jnp.sum(grad_act2, axis=(0, 1))
    grad_middle = out_cotangent + norm_back(grad_act2, normed2, inv2, ln2_gain)
    grad_mid_b = grad_middle.astype(bf16)
    out_grad = matmul("cld,cle->de", mixed, grad_mid_b)
    out_bias_grad = jnp.sum(grad_middle, axis=(0, 1))
    grad_mixed = matmul("cle,de->cld", grad_mid_b, attn_out).astype(bf16).reshape(heads_shape)
    again = jnp.exp(matmul("clhe,cmhe->chlm", query, keys) - log_total)
    grad_probs = matmul("clhe,cmhe->chlm", grad_mixed, values)
    inner = jnp.sum(again * grad_probs, axis=-1, keepdims=True)
    grad_scores = (again * (grad_probs - inner)).astype(bf16)
    grad_query = matmul("chlm,cmhe->clhe", grad_scores, keys).reshape(clips, frames, width) * scale
    grad_keys = matmul("chlm,clhe->cmhe", grad_scores, query).reshape(clips, frames, width)
    grad_values = matmul("chlm,clhe->cmhe", again.astype(bf16), grad_mixed).reshape(
        clips, frames, width
    )
    query_bias_grad = jnp.sum(grad_query, axis=(0, 1))
    value_bias_grad = jnp.sum(grad_values, axis=(0, 1))
    grad_query_b = grad_query.astype(bf16)
    grad_keys_b = grad_keys.astype(bf16)
    grad_values_b = grad_values.astype(bf16)
    joined = jnp.concatenate((grad_query_b, grad_keys_b, grad_values_b), axis=-1)
    qkv_grad = matmul("cld,cle->de", act1, joined)
    grad_act1 = matmul("cle,de->cld", joined, attn_qkv)
    ln1_gain_grad = jnp.sum(grad_act1 * normed1, axis=(0, 1))
    ln1_bias_grad = jnp.sum(grad_act1, axis=(0, 1))
    input_grad = grad_middle + norm_back(grad_act1, normed1, inv1, ln1_gain)
    attn_grads = (
        ln1_gain_grad,
        ln1_bias_grad,
        qkv_grad,
        query_bias_grad,
        value_bias_grad,
        out_grad,
        out_bias_grad,
    )
    mlp_grads = (ln2_gain_grad, ln2_bias_grad, fc1_grad, fc1_bias_grad, fc2_grad, fc2_bias_grad)
    return (input_grad, attn_grads, mlp_grads)


LANES = 128


def turn(value, step):
    count = lax.axis_size("replica")
    return lax.ppermute(value, "replica", [(i, (i + step) % count) for i in range(count)])


def piece_width(width):
    return LANES * (2 * width // (3 * LANES * lax.axis_size("replica")))


def gathered(weight):
    return lax.all_gather(weight, "shard", axis=0, tiled=True)


def scattered(value):
    return lax.psum_scatter(value, "shard", scatter_dimension=0, tiled=True)


def replica_sum(part):
    count = lax.axis_size("replica")
    total = part.astype(jnp.float32)
    for step in range(1, count):
        total = total + turn(part, step).astype(jnp.float32)
    return total


def owned(grad):
    return replica_sum(scattered(grad.astype(jnp.bfloat16)))


def body(
    block_input,
    out_cotangent,
    ln1_gain,
    ln1_bias,
    attn_query,
    query_bias,
    attn_key,
    attn_value,
    value_bias,
    attn_out,
    out_bias,
    ln2_gain,
    ln2_bias,
    fc1_weight,
    fc1_bias,
    fc2_weight,
    fc2_bias,
):
    f32 = jnp.float32
    bf16 = jnp.bfloat16
    rows, width = attn_query.shape
    per_row = fc1_bias.shape[0] // rows
    narrow = (
        ln1_gain,
        ln1_bias,
        query_bias,
        value_bias,
        out_bias,
        ln2_gain,
        ln2_bias,
        fc2_bias,
    )
    columns = jnp.concatenate(
        (jnp.stack(narrow, axis=1), fc1_bias.reshape(rows, per_row)), axis=1
    )
    used = columns.shape[1]
    spare = -used % 128
    packed = jnp.concatenate(
        (attn_query, attn_key, attn_value, attn_out, jnp.pad(columns, ((0, 0), (0, spare)))),
        axis=1,
    )
    attn_all = gathered(packed)
    fc1_all = gathered(fc1_weight)
    fc2_all = gathered(fc2_weight)
    small = attn_all[:, 4 * width : 4 * width + used]
    g1, b1, bq, bv, bo, g2, b2, bf2 = (small[:, i] for i in range(len(narrow)))
    bf1 = small[:, len(narrow) :].reshape(-1)
    attn_full = (g1, b1, attn_all[:, : 3 * width], bq, bv, attn_all[:, 3 * width : 4 * width], bo)
    mlp_full = (g2, b2, fc1_all, bf1, fc2_all, bf2)
    block_output, saved = forward_pass(block_input, attn_full, mlp_full)
    input_grad, attn_grads, mlp_grads = backward_pass(out_cotangent, saved, attn_full, mlp_full)
    dg1, db1, dqkv, dbq, dbv, dout, dbo = attn_grads
    dg2, db2, dfc1, dbf1, dfc2, dbf2 = mlp_grads

    fc2_owned = owned(dfc2)
    fc1_owned = owned(dfc1)
    thin = jnp.concatenate(
        (
            jnp.stack((dg1, db1, dbq, dbv, dbo, dg2, db2, dbf2), axis=1),
            dbf1.reshape(-1, per_row),
        ),
        axis=1,
    )
    attn_owned = owned(
        jnp.concatenate((dqkv, dout, jnp.pad(thin, ((0, 0), (0, spare)))), axis=1)
    )
    base = 4 * width
    og1, ob1, obq, obv, obo, og2, ob2, obf2 = (
        attn_owned[:, base + i] for i in range(len(narrow))
    )
    obf1 = attn_owned[:, base + len(narrow) : base + used].reshape(-1)
    return (
        block_output,
        input_grad,
        og1,
        ob1,
        attn_owned[:, :width],
        obq,
        attn_owned[:, width : 2 * width],
        attn_owned[:, 2 * width : 3 * width],
        obv,
        attn_owned[:, 3 * width : 4 * width],
        obo,
        og2,
        ob2,
        fc1_owned,
        obf1,
        fc2_owned,
        obf2,
    )


def solution(mesh):
    placed = (
        P(("replica", "shard"), None, None),
        P(("replica", "shard"), None, None),
        P("shard"),
        P("shard"),
        P("shard", None),
        P("shard"),
        P("shard", None),
        P("shard", None),
        P("shard"),
        P("shard", None),
        P("shard"),
        P("shard"),
        P("shard"),
        P("shard", None),
        P("shard"),
        P("shard", None),
        P("shard"),
    )
    return jax.shard_map(
        body,
        mesh=mesh,
        in_specs=placed,
        out_specs=(
            P(("replica", "shard"), None, None),
            P(("replica", "shard"), None, None),
            P("shard"),
            P("shard"),
            P("shard", None),
            P("shard"),
            P("shard", None),
            P("shard", None),
            P("shard"),
            P("shard", None),
            P("shard"),
            P("shard"),
            P("shard"),
            P("shard", None),
            P("shard"),
            P("shard", None),
            P("shard"),
        ),
        check_vma=False,
    )
```
